128 devices in a mesh: seq: 16 (over y, z), blk: 8 (over x, core).
Axes of the slice: x: 4, y: 4, z: 4, core: 2. Of those that a mesh axis runs over, the one named last changes fastest.
Arguments:
- tokens: bfloat16 [8192, 6144], P(('seq', 'blk')), may hold values from -6 to 6
- norm_gain: float32 [6144], replicated, may hold values from 0.1 to 1.9
- qkv_weight: bfloat16 [6144, 3, 3072], P('seq', None, 'blk'), may hold values from -0.078125 to 0.078125
- out_weight: bfloat16 [3072, 6144], P('blk', 'seq'), may hold values from -0.109375 to 0.109375
- log_decay: float32 [8192, 24], P('seq', 'blk'), may hold values from -2 to 0, as said below
Outputs:
- layer_out: bfloat16 [8192, 6144], P(('seq', 'blk'))
The draws below stay inside these ranges and needn't reach their ends.
Inputs may be any that keep to these rules, and one draw needn't show every extreme that they name: log_decay is negative.
All inputs are finite; a program needn't handle non-finite values.
Results may differ from the reference program's by a relative error of at most 0.013.
Values may be sent and summed in bfloat16 or wider, within the bound.
No kernel may reach another device: no remote copies, remote signals or barrier semaphores. Data moves between devices by JAX's collectives and lax.ppermute only.
A program may use at most 128 MiB of HBM per device.

```python
import jax
import jax.numpy as jnp
from jax import lax

D = 6144
H = 24
DH = 128
TOK_DEV = 64
SECTION = 512
TOTAL_STEP_COUNT = 8192
N_SEQ = 16
N_BLK = 8


def draw_log_decay(key, part):
    lookup_vectors_ordered = jax.random.split(key, 7)
    slow_share = 0.5
    slow_heads = jax.random.uniform(lookup_vectors_ordered[0], (H,)) < slow_share
    fast_span = jax.random.uniform(lookup_vectors_ordered[1], (H,), jnp.float32, 30.0, 50.0)
    slow_span = TOTAL_STEP_COUNT * jax.random.uniform(lookup_vectors_ordered[2], (H,), jnp.float32, 1.5, 4.0)
    interval_extents = jnp.where(slow_heads, slow_span, fast_span)
    section_factor = jax.random.uniform(lookup_vectors_ordered[3], (TOTAL_STEP_COUNT // SECTION,), jnp.float32, 0.6, 1.6)
    element_indices = jnp.arange(TOTAL_STEP_COUNT)
    forgetting_multipliers = jnp.take(section_factor, element_indices // SECTION)
    record_irregularity = jax.random.uniform(lookup_vectors_ordered[4], (TOTAL_STEP_COUNT, H), jnp.float32, 0.7, 1.4)
    episode_offset = jax.random.randint(lookup_vectors_ordered[5], (3,), 0, TOTAL_STEP_COUNT)
    episode_extent = jnp.log(jax.random.uniform(lookup_vectors_ordered[6], (3,), jnp.float32, 0.65, 0.8))
    episode_catalog = jnp.sum(jnp.where(element_indices[:, None] == episode_offset[None, :], episode_extent[None, :], 0.0), axis=1)
    return -(record_irregularity * forgetting_multipliers[:, None]) / interval_extents[None, :] + episode_catalog[:, None]


def block_levels(key, extent, cuts, least, largest):
    level = 1.0
    for dim, shards_of in cuts:
        heights = jax.random.uniform(jax.random.fold_in(jax.random.fold_in(key, 6), dim), (shards_of,), jnp.float32, least / len(cuts), largest / len(cuts))
        level = level * jnp.repeat(jnp.exp(heights), extent[dim] // shards_of).reshape((-1,) + (1,) * (len(extent) - 1 - dim))
    return level


def gaussian(own_key, shape, deviation, reach, shards=(), dtype=jnp.bfloat16):
    level = block_levels(own_key, shape, shards, -0.22, 0.18) if shards else 1.0
    entries = jax.random.normal(own_key, shape, jnp.float32) * deviation * level
    return jnp.minimum(jnp.maximum(entries, -reach), reach).astype(dtype)


def setup_inputs(seed: int = 0) -> dict:
    splits = jax.random.split(jax.random.key(seed), 6)
    return {
        "tokens": gaussian(splits[0], (TOTAL_STEP_COUNT, D), 1.0, 6.0, ((0, 128),)),
        "norm_gain": jnp.clip(1.0 + 0.18 * jax.random.normal(splits[1], (D,), jnp.float32), 0.1, 1.9),
        "qkv_weight": gaussian(splits[2], (D, 3, H * DH), D ** -0.5, 0.078125, ((0, 16), (2, 8))),
        "out_weight": gaussian(splits[3], (H * DH, D), (H * DH) ** -0.5, 0.109375, ((0, 8), (1, 16))),
        "log_decay": draw_log_decay(jax.random.fold_in(splits[5], 71), 0),
    }


eps_norm = 1e-05

def reference(tokens, norm_gain, qkv_weight, out_weight, log_decay):
    section_len = TOK_DEV * N_BLK
    per_group = H // N_BLK
    inv_root = DH ** (-0.5)
    token_sections = tokens.reshape(N_SEQ, section_len, D)
    decay_sections = log_decay.reshape(N_SEQ, section_len, H)
    flat_weight = qkv_weight.reshape(D, 3 * H * DH)
    group_weight = out_weight.reshape(N_BLK, per_group * DH, D).astype(jnp.float32)
    element_indices = jnp.arange(section_len)
    causal = (element_indices[:, None] >= element_indices[None, :])[:, :, None]
    highest = lax.Precision.HIGHEST

    def one_section(state, inputs):
        section_x, section_decay = inputs
        wide_x = section_x.astype(jnp.float32)
        mean_sq = lax.optimization_barrier(jnp.mean(wide_x * wide_x, axis=-1, keepdims=True))
        normed_x = (wide_x * lax.rsqrt(mean_sq + eps_norm) * norm_gain.astype(jnp.float32)).astype(jnp.bfloat16)
        projected = jnp.dot(normed_x, flat_weight, preferred_element_type=jnp.float32).astype(jnp.bfloat16)
        projected = projected.reshape(section_len, 3, H, DH).astype(jnp.float32)
        queries = projected[:, 0]
        keys_all = projected[:, 1]
        values_all = projected[:, 2]
        cum_log = jnp.cumsum(section_decay, axis=0)
        diffs = cum_log[:, None, :] - cum_log[None, :, :]
        decays = jnp.where(causal, jnp.exp(jnp.where(causal, diffs, 0.0)), 0.0)
        scores = jnp.einsum('thd,shd->tsh', queries, keys_all, precision=highest)
        pair = (scores * decays * inv_root).astype(jnp.bfloat16)
        pair = lax.optimization_barrier(pair).astype(jnp.float32)
        intra = jnp.einsum('tsh,shd->thd', pair, values_all, precision=highest)
        cross = jnp.exp(cum_log)[:, :, None] * inv_root * jnp.einsum('thd,hde->the', queries, state, precision=highest)
        mixed = intra + cross
        mixed_sq = lax.optimization_barrier(jnp.mean(mixed * mixed, axis=-1, keepdims=True))
        heads_out = (mixed * lax.rsqrt(mixed_sq + eps_norm)).astype(jnp.bfloat16)
        heads_out = lax.optimization_barrier(heads_out).astype(jnp.float32)
        grouped = heads_out.reshape(section_len, N_BLK, per_group * DH)
        partials = jnp.einsum('tgc,gcd->gtd', grouped, group_weight, precision=highest).astype(jnp.bfloat16)
        partials = lax.optimization_barrier(partials).astype(jnp.float32)
        output = (wide_x + lax.optimization_barrier(jnp.sum(partials, axis=0))).astype(jnp.bfloat16)
        last_log = cum_log[-1]
        carried = jnp.exp(last_log[None, :] - cum_log)
        summary = jnp.einsum('sh,shd,she->hde', carried, keys_all, values_all, precision=highest)
        new_state = jnp.exp(last_log)[:, None, None] * state + summary
        return (new_state, output)
    initial = jnp.zeros((H, DH, DH), jnp.float32)
    _, outputs = lax.scan(one_section, initial, (token_sections, decay_sections))
    return outputs.reshape(N_SEQ * section_len, D)
```

```python
import jax
import jax.numpy as jnp
from jax import lax
from jax.sharding import PartitionSpec as P

DH = 128
eps_norm = 1e-05


def z_shift(k):
    return "seq", [(y * 4 + z, y * 4 + (z + k) % 4) for y in range(4) for z in range(4)]


def y_shift(k):
    return "seq", [(y * 4 + z, ((y + k) % 4) * 4 + z) for y in range(4) for z in range(4)]


def x_shift(k):
    return "blk", [(x * 2 + c, ((x + k) % 4) * 2 + c) for x in range(4) for c in range(2)]


PARTNER = ("blk", [(b, b ^ 1) for b in range(8)])
SLOT = (0, 1, 3, 2)


def send(a, to):
    return lax.ppermute(a, *to)


def ring_gather(a, shift):
    half = a.shape[0] // 2
    before = send(a, shift(1))
    after = send(a, shift(-1))
    far_lo = send(before[:half], shift(1))
    far_hi = send(after[half:], shift(-1))
    return jnp.concatenate([a, before, after, far_lo, far_hi], axis=0)


def plane_gather(a, first, second):
    return ring_gather(ring_gather(a, first), second)


def on_device(tokens, norm_gain, qkv_weight, out_weight, log_decay):
    highest = lax.Precision.HIGHEST
    f32, bf16 = jnp.float32, jnp.bfloat16
    inv_root = DH ** (-0.5)
    rows, width = tokens.shape
    k_len, _, head_width = qkv_weight.shape
    local_heads = head_width // DH
    section_len = rows * 8
    place = lax.axis_index("seq")
    y, z = place // 4, place % 4
    blk = lax.axis_index("blk")
    x, core = blk // 2, blk % 2
    lag = jnp.arange(4)
    slot = jnp.array(SLOT)
    y_back, z_back = slot[(y - lag) % 4], slot[(z - lag) % 4]

    w_kv = lax.all_gather(
        jnp.concatenate([qkv_weight[:, 1], qkv_weight[:, 2]], axis=1), "seq", axis=0, tiled=True
    )
    w_q = lax.all_gather(qkv_weight[:, 0], "seq", axis=0, tiled=True)

    wide = tokens.astype(f32)
    mean_sq = jnp.mean(wide * wide, axis=-1, keepdims=True)
    normed = (wide * lax.rsqrt(mean_sq + eps_norm) * norm_gain).astype(bf16)
    mine = jnp.stack([normed] + [send(normed, x_shift(k)) for k in (1, 2, 3)])
    relative = jnp.stack([mine, send(mine, PARTNER)])
    ids = jnp.arange(8)
    section = relative[(ids % 2) ^ core, (x - ids // 2) % 4].reshape(section_len, width)

    cum_log = jnp.cumsum(log_decay, axis=0)
    last_log = cum_log[-1]

    tri = head_width // 3
    hk = head_width // 2
    t_hi = lax.reduce_precision(last_log, 8, 7)
    t_mid = lax.reduce_precision(last_log - t_hi, 8, 7)
    t_lo = last_log - t_hi - t_mid
    tot = jnp.stack([t_hi, t_mid, t_lo], axis=1).astype(bf16).reshape(3 * local_heads, 1)
    tot = jnp.pad(jnp.broadcast_to(tot, (3 * local_heads, tri)), ((0, 16 - 3 * local_heads), (0, 0)))
    o_a = jnp.concatenate([out_weight[:, :tri], out_weight[:hk, 2 * tri :], tot], axis=0)
    o_b = jnp.concatenate([out_weight[:, tri : 2 * tri], out_weight[hk:, 2 * tri :]], axis=0)
    blocks_a = plane_gather(o_a, y_shift, z_shift).reshape(4, 4, -1, tri)[z_back][:, y_back]
    blocks_a = blocks_a.transpose(1, 0, 2, 3)
    blocks_b = plane_gather(o_b, z_shift, y_shift).reshape(4, 4, -1, tri)[y_back][:, z_back]
    third = jnp.concatenate(
        [blocks_a[:, :, head_width : head_width + hk], blocks_b[:, :, head_width:]], axis=2
    )
    out_full = jnp.stack([blocks_a[:, :, :head_width], blocks_b[:, :, :head_width], third], axis=2)
    out_full = out_full.transpose(3, 0, 1, 2, 4).reshape(head_width, 16 * head_width)
    totals = blocks_a[:, :, head_width + hk : head_width + hk + 3 * local_heads, 0].astype(f32)
    by_yz = totals.reshape(4, 4, local_heads, 3).sum(axis=-1)
    by_z = lax.dynamic_index_in_dim(by_yz, y, 0, False)
    row_tot = by_yz.sum(axis=1)

    head_log = cum_log.T
    steps = jnp.arange(section_len)
    causal = (steps[:, None] >= steps[None, :])[None, :, :]
    diffs = head_log[:, :, None] - head_log[:, None, :]
    decays = jnp.where(causal, jnp.exp(jnp.where(causal, diffs, 0.0)), 0.0)
    carried = jnp.exp(last_log[None, :] - cum_log)

    def coefs(totals, upto):
        inside = (lag[None, :] > lag[:, None]) & (lag[None, :] < upto)
        sums = jnp.where(inside[:, :, None], totals[None], 0.0).sum(axis=1)
        return jnp.where((lag < upto)[:, None], jnp.exp(sums), 0.0)

    c_row = coefs(by_z, 4)[(z - lag) % 4]
    c_in = coefs(by_z, z)[(z - lag) % 4]
    c_y = coefs(row_tot, y)[(y - lag) % 4]
    lead = jnp.exp(jnp.where((lag < z)[:, None], by_z, 0.0).sum(axis=0))
    c_y = c_y * lead[None]

    proj_kv = jnp.dot(section, w_kv, preferred_element_type=f32).astype(bf16)
    keys = proj_kv[:, :head_width].reshape(section_len, local_heads, DH)
    values = proj_kv[:, head_width:].reshape(section_len, local_heads, DH)
    weighted_keys = keys.astype(f32) * carried[:, :, None]
    summary = jnp.einsum("shd,she->hde", weighted_keys, values.astype(f32), precision=highest)

    sum_bf = summary.astype(bf16)
    sums_z = [summary] + [send(sum_bf, z_shift(k)).astype(f32) for k in (1, 2, 3)]
    row_state = sum(c_row[k][:, None, None] * sums_z[k] for k in range(4))
    state_in = sum(c_in[k][:, None, None] * sums_z[k] for k in range(4))
    row_bf = row_state.astype(bf16)
    for k in (1, 2, 3):
        state_in = state_in + c_y[k][:, None, None] * send(row_bf, y_shift(k)).astype(f32)

    w_q, state_in, out_full = lax.optimization_barrier((w_q, state_in, out_full))
    queries = jnp.dot(section, w_q, preferred_element_type=f32).astype(bf16)
    queries = queries.reshape(section_len, local_heads, DH)
    scores = jnp.einsum("thd,shd->hts", queries, keys, preferred_element_type=f32)
    pair = (scores * decays * inv_root).astype(bf16)
    intra = jnp.einsum("hts,shd->thd", pair, values, preferred_element_type=f32)
    cross = (
        jnp.exp(cum_log)[:, :, None]
        * inv_root
        * jnp.einsum("thd,hde->the", queries.astype(f32), state_in, precision=highest)
    )
    mixed = intra + cross
    mixed_sq = jnp.mean(mixed * mixed, axis=-1, keepdims=True)
    heads_out = (mixed * lax.rsqrt(mixed_sq + eps_norm)).astype(bf16).reshape(section_len, head_width)
    summed = lax.psum_scatter(
        jnp.dot(heads_out, out_full, preferred_element_type=f32).astype(bf16),
        "blk",
        scatter_dimension=0,
        tiled=True,
    ).astype(f32)
    return (tokens.astype(f32) + summed).astype(bf16)


def solution(mesh):
    in_specs = (
        P(("seq", "blk"), None),
        P(),
        P("seq", None, "blk"),
        P("blk", "seq"),
        P("seq", "blk"),
    )
    out_specs = P(("seq", "blk"), None)
    return jax.shard_map(
        on_device, mesh=mesh, in_specs=in_specs, out_specs=out_specs, check_vma=False
    )
```

```python
import jax
import jax.numpy as jnp
from jax import lax
from jax.experimental import pallas as pl
from jax.experimental.pallas import tpu as pltpu
from jax.sharding import PartitionSpec as P

DH = 128
eps_norm = 1e-05


def z_shift(k):
    return "seq", [(y * 4 + z, y * 4 + (z + k) % 4) for y in range(4) for z in range(4)]


def y_shift(k):
    return "seq", [(y * 4 + z, ((y + k) % 4) * 4 + z) for y in range(4) for z in range(4)]


def x_shift(k):
    return "blk", [(x * 2 + c, ((x + k) % 4) * 2 + c) for x in range(4) for c in range(2)]


PARTNER = ("blk", [(b, b ^ 1) for b in range(8)])
VMEM = pl.BlockSpec(memory_space=pltpu.VMEM)


def send(a, to):
    return lax.ppermute(a, *to)


def ring_gather(a, shift):
    half = a.shape[0] // 2
    before = send(a, shift(1))
    after = send(a, shift(3))
    return [a, before, after, send(before[:half], shift(1)), send(after[half:], shift(3))]


def stack_pairs(*rings):
    rows, width = rings[0][0].shape
    n = len(rings)

    def body(*refs):
        for r in range(n):
            own, before, after, far_lo, far_hi = refs[5 * r : 5 * r + 5]
            lo, hi = refs[5 * n + 2 * r : 5 * n + 2 * r + 2]
            lo[0], lo[1] = own[...], before[...]
            hi[0] = after[...]
            hi[1, : rows // 2] = far_lo[...]
            hi[1, rows // 2 :] = far_hi[...]

    shape = jax.ShapeDtypeStruct((2, rows, width), rings[0][0].dtype)
    return pl.pallas_call(
        body,
        out_shape=[shape] * (2 * n),
        in_specs=[VMEM] * (5 * n),
        out_specs=[VMEM] * (2 * n),
        name="stack_pairs",
        compiler_params=pltpu.CompilerParams(vmem_limit_bytes=8 * 1024 * 1024),
    )(*(a for ring in rings for a in ring))


def assemble(mine, theirs):
    rows, width = mine[0].shape

    def body(*refs):
        out = refs[8]
        blk = lax.axis_index("blk")
        x, core = blk // 2, blk % 2
        for k in range(4):
            chip = (x + 4 - k) % 4
            for ref, c in ((refs[k], core), (refs[4 + k], 1 - core)):
                out[pl.ds(pl.multiple_of((chip * 2 + c) * rows, rows), rows)] = ref[...]

    return pl.pallas_call(
        body,
        out_shape=jax.ShapeDtypeStruct((8 * rows, width), mine[0].dtype),
        in_specs=[VMEM] * 8,
        out_specs=VMEM,
        name="assemble",
        compiler_params=pltpu.CompilerParams(vmem_limit_bytes=16 * 1024 * 1024),
    )(*mine, *theirs)


NEAR = ((0, 0, 1), (0, 3, 2), (1, 0, 1), (1, 3, 2), (3, 0, 1), (3, 3, 2))
FAR = ((2, 0, 1), (2, 3, 2))


def partial_kv(section, k_pieces, v_pieces, plan, sums=None):
    t_len, (_, k_len, n_len) = section.shape[0], k_pieces[0].shape
    n = len(plan)

    def body(*refs):
        x_ref, ks, vs = refs[0], refs[1 : 1 + n], refs[1 + n : 1 + 2 * n]
        k_out, v_out = refs[-2:]
        place = lax.axis_index("seq")
        y, z = place // 4, place % 4

        def total(pieces, owner):
            acc = None
            for ref, (second, *firsts) in zip(pieces, plan, strict=True):
                for i, first in enumerate(firsts):
                    at = owner(first, second) * k_len
                    cols = x_ref[:, pl.ds(pl.multiple_of(at, 128), k_len)]
                    dot = jnp.dot(cols, ref[i], preferred_element_type=jnp.float32)
                    acc = dot if acc is None else acc + dot
            return acc

        k_sum = total(ks, lambda f, s: ((y + 4 - f) % 4) * 4 + (z + 4 - s) % 4)
        v_sum = total(vs, lambda f, s: ((y + 4 - s) % 4) * 4 + (z + 4 - f) % 4)
        if sums is not None:
            k_sum, v_sum = k_sum + refs[1 + 2 * n][...], v_sum + refs[2 + 2 * n][...]
        k_out[...] = k_sum.astype(k_out.dtype)
        v_out[...] = v_sum.astype(v_out.dtype)

    extra = () if sums is None else tuple(sums)
    out = jax.ShapeDtypeStruct((t_len, n_len), jnp.float32 if sums is None else jnp.bfloat16)
    return pl.pallas_call(
        body,
        out_shape=[out, out],
        in_specs=[VMEM] * (1 + 2 * n + len(extra)),
        out_specs=[VMEM] * 2,
        name="kv_near" if sums is None else "kv_far",
        compiler_params=pltpu.CompilerParams(vmem_limit_bytes=36 * 1024 * 1024),
    )(section, *k_pieces, *v_pieces, *extra)


STEP = 4


def project_q(section, w_qo):
    n_seq, k_len, n_len = w_qo.shape[0], w_qo.shape[1] // 2, w_qo.shape[2]
    t_len = section.shape[0]
    last = n_seq // STEP - 1

    def body(x_ref, w_ref, out, acc):
        total = None
        for i in range(STEP):
            dot = jnp.dot(x_ref[:, i * k_len : (i + 1) * k_len], w_ref[i], preferred_element_type=jnp.float32)
            total = dot if total is None else total + dot

        @pl.when(pl.program_id(0) == 0)
        def _():
            acc[...] = total

        @pl.when(pl.program_id(0) > 0)
        def _():
            acc[...] += total

        @pl.when(pl.program_id(0) == last)
        def _():
            out[...] = acc[...].astype(out.dtype)

    return pl.pallas_call(
        body,
        grid=(n_seq // STEP,),
        out_shape=jax.ShapeDtypeStruct((t_len, n_len), jnp.bfloat16),
        in_specs=[
            pl.BlockSpec((t_len, STEP * k_len), lambda s: (0, s)),
            pl.BlockSpec((STEP, k_len, n_len), lambda s: (s, 0, 0)),
        ],
        out_specs=pl.BlockSpec((t_len, n_len), lambda s: (0, 0)),
        scratch_shapes=[pltpu.VMEM((t_len, n_len), jnp.float32)],
        name="project_q",
        compiler_params=pltpu.CompilerParams(vmem_limit_bytes=56 * 1024 * 1024),
    )(section, w_qo)


def project_out(heads_out, w_qo):
    n_seq, k_len, n_len = w_qo.shape[0], w_qo.shape[1] // 2, w_qo.shape[2]
    t_len = heads_out.shape[0]

    def body(h_ref, w_ref, out):
        for i in range(STEP):
            dot = jnp.dot(h_ref[...], w_ref[i], preferred_element_type=jnp.float32)
            out[:, i * n_len : (i + 1) * n_len] = dot.astype(out.dtype)

    return pl.pallas_call(
        body,
        grid=(n_seq // STEP,),
        out_shape=jax.ShapeDtypeStruct((t_len, n_seq * n_len), jnp.bfloat16),
        in_specs=[
            pl.BlockSpec((t_len, k_len), lambda s: (0, 0)),
            pl.BlockSpec((STEP, k_len, n_len), lambda s: (s, 1, 0)),
        ],
        out_specs=pl.BlockSpec((t_len, STEP * n_len), lambda s: (0, s)),
        name="project_out",
        compiler_params=pltpu.CompilerParams(vmem_limit_bytes=58 * 1024 * 1024),
    )(heads_out, w_qo)


def row_weights(tots):
    def body(*refs):
        ins, (in_ref, row_ref, lead_ref, sum_ref) = refs[:4], refs[4:]
        z = lax.axis_index("seq") % 4
        tot = [r[...] for r in ins]

        def over(keep):
            return sum(jnp.where(keep(j), tot[j], 0.0) for j in range(4))

        for k in range(4):
            at = (z + 4 - k) % 4
            in_ref[k] = jnp.where(at < z, jnp.exp(over(lambda j: ((z + 4 - j) % 4 > at) & ((z + 4 - j) % 4 < z))), 0.0)
            row_ref[k] = jnp.exp(over(lambda j: (z + 4 - j) % 4 > at))
        lead_ref[...] = jnp.exp(over(lambda j: (z + 4 - j) % 4 < z))
        sum_ref[...] = over(lambda j: j >= 0)

    one = jax.ShapeDtypeStruct(tots[0].shape, jnp.float32)
    four = jax.ShapeDtypeStruct((4, *one.shape), jnp.float32)
    return pl.pallas_call(
        body,
        out_shape=[four, four, one, one],
        in_specs=[VMEM] * 4,
        out_specs=[VMEM] * 4,
        name="row_weights",
        compiler_params=pltpu.CompilerParams(vmem_limit_bytes=2 * 1024 * 1024),
    )(*tots)


def rows_weights(sums, lead):
    def body(*refs):
        ins, lead_ref, out = refs[:4], refs[4], refs[5]
        y = lax.axis_index("seq") // 4
        tot = [r[...] for r in ins]
        for k in range(4):
            at = (y + 4 - k) % 4
            log = sum(jnp.where(((y + 4 - j) % 4 > at) & ((y + 4 - j) % 4 < y), tot[j], 0.0) for j in range(4))
            out[k] = jnp.where(at < y, jnp.exp(log), 0.0) * lead_ref[...]

    return pl.pallas_call(
        body,
        out_shape=jax.ShapeDtypeStruct((4, *lead.shape), jnp.float32),
        in_specs=[VMEM] * 5,
        out_specs=VMEM,
        name="rows_weights",
        compiler_params=pltpu.CompilerParams(vmem_limit_bytes=2 * 1024 * 1024),
    )(*sums, lead)


def on_device(tokens, norm_gain, qkv_weight, out_weight, log_decay):
    highest = lax.Precision.HIGHEST
    f32, bf16 = jnp.float32, jnp.bfloat16
    inv_root = DH ** (-0.5)
    rows, width = tokens.shape
    head_width = qkv_weight.shape[2]
    local_heads = head_width // DH
    section_len = rows * 8

    w_qo = jnp.concatenate([qkv_weight[:, 0], out_weight], axis=0)
    w_qo = lax.all_gather(w_qo, "seq", axis=0, tiled=True).reshape(16, *w_qo.shape)

    tot = jnp.broadcast_to(log_decay.sum(axis=0)[:, None], (local_heads, DH))
    c_in, c_row, lead, row_tot = row_weights([tot] + [send(tot, z_shift(k)) for k in (1, 2, 3)])
    c_y = rows_weights([row_tot] + [send(row_tot, y_shift(k)) for k in (1, 2, 3)], lead)

    w_k, w_v = qkv_weight[:, 1], qkv_weight[:, 2]
    first_k, first_v = ring_gather(w_k, y_shift), ring_gather(w_v, z_shift)

    wide = tokens.astype(f32)
    mean_sq = jnp.mean(wide * wide, axis=-1, keepdims=True)
    normed = (wide * lax.rsqrt(mean_sq + eps_norm) * norm_gain).astype(bf16)
    mine = [normed] + [send(normed, x_shift(k)) for k in (1, 2, 3)]

    k_lo, k_hi, v_lo, v_hi = stack_pairs(first_k, first_v)

    def second(lo, hi, shift):
        lo1, hi3 = send(lo, shift(1)), send(hi, shift(3))
        hi1, lo3 = send(hi, shift(1)), send(lo, shift(3))
        return [lo, hi, lo1, hi1, lo3, hi3], [send(lo1, shift(1)), send(hi3, shift(3))]

    near_k, far_k = second(k_lo, k_hi, z_shift)
    near_v, far_v = second(v_lo, v_hi, y_shift)

    log_decay, mine, _ = lax.optimization_barrier((log_decay, mine, (k_lo, v_lo)))
    theirs = [send(m, PARTNER) for m in mine]
    section = assemble(mine, theirs)

    cum_log = jnp.cumsum(log_decay, axis=0)
    last_log = cum_log[-1]
    head_log = cum_log.T
    steps = jnp.arange(section_len)
    causal = (steps[:, None] >= steps[None, :])[None, :, :]
    diffs = head_log[:, :, None] - head_log[:, None, :]
    decays = jnp.where(causal, jnp.exp(jnp.where(causal, diffs, 0.0)), 0.0)
    carried = jnp.exp(last_log[None, :] - cum_log)

    sums = partial_kv(section, near_k, near_v, NEAR)
    keys, values = partial_kv(section, far_k, far_v, FAR, sums)
    keys = keys.reshape(section_len, local_heads, DH)
    values = values.reshape(section_len, local_heads, DH)
    weighted_keys = keys.astype(f32) * carried[:, :, None]
    summary = jnp.einsum("shd,she->hde", weighted_keys, values.astype(f32), precision=highest)

    sum_bf = summary.astype(bf16)
    sums_z = [summary] + [send(sum_bf, z_shift(k)).astype(f32) for k in (1, 2, 3)]
    row_state = sum(c_row[k][:, None] * sums_z[k] for k in range(4))
    state_in = sum(c_in[k][:, None] * sums_z[k] for k in range(4))
    row_bf = row_state.astype(bf16)
    for k in (1, 2, 3):
        state_in = state_in + c_y[k][:, None] * send(row_bf, y_shift(k)).astype(f32)

    queries = project_q(section, w_qo).reshape(section_len, local_heads, DH)
    scores = jnp.einsum("thd,shd->hts", queries, keys, preferred_element_type=f32)
    pair = (scores * decays * inv_root).astype(bf16)
    intra = jnp.einsum("hts,shd->thd", pair, values, preferred_element_type=f32)
    cross = (
        jnp.exp(cum_log)[:, :, None]
        * inv_root
        * jnp.einsum("thd,hde->the", queries.astype(f32), state_in, precision=highest)
    )
    mixed = intra + cross
    mixed_sq = jnp.mean(mixed * mixed, axis=-1, keepdims=True)
    heads_out = (mixed * lax.rsqrt(mixed_sq + eps_norm)).astype(bf16).reshape(section_len, head_width)
    summed = lax.psum_scatter(
        project_out(heads_out, w_qo), "blk", scatter_dimension=0, tiled=True
    ).astype(f32)
    return (tokens.astype(f32) + summed).astype(bf16)


def solution(mesh):
    in_specs = (
        P(("seq", "blk"), None),
        P(),
        P("seq", None, "blk"),
        P("blk", "seq"),
        P("seq", "blk"),
    )
    out_specs = P(("seq", "blk"), None)
    return jax.shard_map(
        on_device, mesh=mesh, in_specs=in_specs, out_specs=out_specs, check_vma=False
    )
```

```python
import jax
import jax.numpy as jnp
from jax import lax
from jax.experimental import pallas as pl
from jax.experimental.pallas import tpu as pltpu
from jax.sharding import PartitionSpec as P


DH = 128
eps_norm = 1e-05


def z_shift(k):
    return "seq", [(y * 4 + z, y * 4 + (z + k) % 4) for y in range(4) for z in range(4)]


def y_shift(k):
    return "seq", [(y * 4 + z, ((y + k) % 4) * 4 + z) for y in range(4) for z in range(4)]


def x_shift(k):
    return "blk", [(x * 2 + c, ((x + k) % 4) * 2 + c) for x in range(4) for c in range(2)]


PARTNER = ("blk", [(b, b ^ 1) for b in range(8)])
VMEM = pl.BlockSpec(memory_space=pltpu.VMEM)


def send(a, to):
    return lax.ppermute(a, *to)


def ring_gather(a, shift):
    half = a.shape[0] // 2
    before = send(a, shift(1))
    after = send(a, shift(3))
    return [a, before, after, send(before[:half], shift(1)), send(after[half:], shift(3))]


def stack_pairs(*rings):
    rows, width = rings[0][0].shape
    n = len(rings)

    def body(*refs):
        for r in range(n):
            own, before, after, far_lo, far_hi = refs[5 * r : 5 * r + 5]
            lo, hi = refs[5 * n + 2 * r : 5 * n + 2 * r + 2]
            lo[0], lo[1] = own[...], before[...]
            hi[0] = after[...]
            hi[1, : rows // 2] = far_lo[...]
            hi[1, rows // 2 :] = far_hi[...]

    shape = jax.ShapeDtypeStruct((2, rows, width), rings[0][0].dtype)
    return pl.pallas_call(
        body,
        out_shape=[shape] * (2 * n),
        in_specs=[VMEM] * (5 * n),
        out_specs=[VMEM] * (2 * n),
        name="stack_pairs",
        compiler_params=pltpu.CompilerParams(vmem_limit_bytes=8 * 1024 * 1024),
    )(*(a for ring in rings for a in ring))


def assemble(mine, theirs):
    rows, width = mine[0].shape

    def body(*refs):
        out = refs[8]
        blk = lax.axis_index("blk")
        x, core = blk // 2, blk % 2
        for k in range(4):
            chip = (x + 4 - k) % 4
            for ref, c in ((refs[k], core), (refs[4 + k], 1 - core)):
                out[pl.ds(pl.multiple_of((chip * 2 + c) * rows, rows), rows)] = ref[...]

    return pl.pallas_call(
        body,
        out_shape=jax.ShapeDtypeStruct((8 * rows, width), mine[0].dtype),
        in_specs=[VMEM] * 8,
        out_specs=VMEM,
        name="assemble",
        compiler_params=pltpu.CompilerParams(vmem_limit_bytes=16 * 1024 * 1024),
    )(*mine, *theirs)


NEAR = ((0, 0, 1), (0, 3, 2), (1, 0, 1), (1, 3, 2), (3, 0, 1), (3, 3, 2))
FAR = ((2, 0, 1), (2, 3, 2))


def partial_kv(section, k_pieces, v_pieces, plan, sums=None):
    t_len, (_, k_len, n_len) = section.shape[0], k_pieces[0].shape
    n = len(plan)

    def body(*refs):
        x_ref, ks, vs = refs[0], refs[1 : 1 + n], refs[1 + n : 1 + 2 * n]
        k_out, v_out = refs[-2:]
        place = lax.axis_index("seq")
        y, z = place // 4, place % 4
        half = t_len // 2

        def total(pieces, owner, rows, start, out):
            acc = None if start is None else start[rows]
            for ref, (second, *firsts) in zip(pieces, plan, strict=True):
                for i, first in enumerate(firsts):
                    at = owner(first, second) * k_len
                    cols = x_ref[rows, pl.ds(pl.multiple_of(at, 128), k_len)]
                    dot = jnp.dot(cols, ref[i], preferred_element_type=jnp.float32)
                    acc = dot if acc is None else acc + dot
            out[rows] = acc.astype(out.dtype)

        starts = (None, None) if sums is None else (refs[1 + 2 * n], refs[2 + 2 * n])

        def one(r, carry):
            rows = pl.ds(pl.multiple_of(r * half, 8), half)
            total(ks, lambda f, s: ((y + 4 - f) % 4) * 4 + (z + 4 - s) % 4, rows, starts[0], k_out)
            total(vs, lambda f, s: ((y + 4 - s) % 4) * 4 + (z + 4 - f) % 4, rows, starts[1], v_out)
            return carry

        lax.fori_loop(0, 2, one, 0)

    extra = () if sums is None else tuple(sums)
    out = jax.ShapeDtypeStruct((t_len, n_len), jnp.float32 if sums is None else jnp.bfloat16)
    return pl.pallas_call(
        body,
        out_shape=[out, out],
        in_specs=[VMEM] * (1 + 2 * n + len(extra)),
        out_specs=[VMEM] * 2,
        name="kv_near" if sums is None else "kv_far",
        compiler_params=pltpu.CompilerParams(vmem_limit_bytes=36 * 1024 * 1024),
    )(section, *k_pieces, *v_pieces, *extra)


def heads_out_dots(pieces, weights, sums=None):
    t_len, _ = pieces[0][2].shape
    n_len = 2 * weights.shape[2]
    n, rows = len(pieces), t_len // 8

    def body(*refs):
        w_ref = refs[n]
        blk = lax.axis_index("blk")
        x, core = blk // 2, blk % 2
        total = refs[-1]

        half = t_len // 2

        def one(i, carry):
            side = i % 2
            block = pl.ds(pl.multiple_of((i // 2) * half, 8), half)
            cols = pl.ds(pl.multiple_of(side * (n_len // 2), 128), n_len // 2)
            acc = None if sums is None else refs[n + 1][block, cols]
            for (back, flip, _), ref in zip(pieces, refs[:n], strict=True):
                owner = ((x + 4 - back) % 4) * 2 + (core + flip) % 2
                dot = jnp.dot(ref[block], w_ref[owner * 2 + side], preferred_element_type=jnp.float32)
                acc = dot if acc is None else acc + dot
            total[block, cols] = acc
            return carry

        lax.fori_loop(0, 4, one, 0)
        if sums is None:
            return
        scratch, outs = total, refs[n + 2 : n + 10]
        for ahead in range(4):
            for flip in range(2):
                to = ((x + ahead) % 4) * 2 + (core + flip) % 2
                part = scratch[pl.ds(pl.multiple_of(to * rows, 8), rows)]
                outs[ahead * 2 + flip][...] = part.astype(jnp.bfloat16)

    if sums is None:
        out_shape = jax.ShapeDtypeStruct((t_len, n_len), jnp.float32)
        out_specs, extra, scratch = VMEM, (), ()
    else:
        out_shape = [jax.ShapeDtypeStruct((rows, n_len), jnp.bfloat16)] * 8
        out_specs, extra, scratch = [VMEM] * 8, (sums,), (pltpu.VMEM((t_len, n_len), jnp.float32),)
    return pl.pallas_call(
        body,
        out_shape=out_shape,
        in_specs=[VMEM] * (n + 1 + len(extra)),
        out_specs=out_specs,
        scratch_shapes=scratch,
        name="out_near" if sums is None else "out_far",
        compiler_params=pltpu.CompilerParams(vmem_limit_bytes=24 * 1024 * 1024),
    )(*(p for _, _, p in pieces), weights, *extra)


def finish(tokens, parts):
    n_len = parts[0].shape[1]

    def body(*refs):
        tok, out = refs[0], refs[9]
        blk = lax.axis_index("blk")
        x, core = blk // 2, blk % 2
        for i in range(8):
            owner = ((x + 4 - i // 2) % 4) * 2 + (core + i % 2) % 2
            cols = pl.ds(pl.multiple_of(owner * n_len, 128), n_len)
            total = tok[:, cols].astype(jnp.float32) + refs[1 + i][...].astype(jnp.float32)
            out[:, cols] = total.astype(out.dtype)

    return pl.pallas_call(
        body,
        out_shape=jax.ShapeDtypeStruct(tokens.shape, tokens.dtype),
        in_specs=[VMEM] * 9,
        out_specs=VMEM,
        name="finish",
        compiler_params=pltpu.CompilerParams(vmem_limit_bytes=8 * 1024 * 1024),
    )(tokens, *parts)


def move_out_weight(out_weight):
    pairs = [(s * 8 + b, (b * 2 + s % 2) * 8 + s // 2) for s in range(16) for b in range(8)]
    return lax.ppermute(out_weight, ("seq", "blk"), pairs)


def row_weights(tots):
    def body(*refs):
        ins, (in_ref, row_ref, lead_ref, sum_ref) = refs[:4], refs[4:]
        z = lax.axis_index("seq") % 4
        tot = [r[...] for r in ins]

        def over(keep):
            return sum(jnp.where(keep(j), tot[j], 0.0) for j in range(4))

        for k in range(4):
            at = (z + 4 - k) % 4
            in_ref[k] = jnp.where(at < z, jnp.exp(over(lambda j: ((z + 4 - j) % 4 > at) & ((z + 4 - j) % 4 < z))), 0.0)
            row_ref[k] = jnp.exp(over(lambda j: (z + 4 - j) % 4 > at))
        lead_ref[...] = jnp.exp(over(lambda j: (z + 4 - j) % 4 < z))
        sum_ref[...] = over(lambda j: j >= 0)

    one = jax.ShapeDtypeStruct(tots[0].shape, jnp.float32)
    four = jax.ShapeDtypeStruct((4, *one.shape), jnp.float32)
    return pl.pallas_call(
        body,
        out_shape=[four, four, one, one],
        in_specs=[VMEM] * 4,
        out_specs=[VMEM] * 4,
        name="row_weights",
        compiler_params=pltpu.CompilerParams(vmem_limit_bytes=2 * 1024 * 1024),
    )(*tots)


def rows_weights(sums, lead):
    def body(*refs):
        ins, lead_ref, out = refs[:4], refs[4], refs[5]
        y = lax.axis_index("seq") // 4
        tot = [r[...] for r in ins]
        for k in range(4):
            at = (y + 4 - k) % 4
            log = sum(jnp.where(((y + 4 - j) % 4 > at) & ((y + 4 - j) % 4 < y), tot[j], 0.0) for j in range(4))
            out[k] = jnp.where(at < y, jnp.exp(log), 0.0) * lead_ref[...]

    return pl.pallas_call(
        body,
        out_shape=jax.ShapeDtypeStruct((4, *lead.shape), jnp.float32),
        in_specs=[VMEM] * 5,
        out_specs=VMEM,
        name="rows_weights",
        compiler_params=pltpu.CompilerParams(vmem_limit_bytes=2 * 1024 * 1024),
    )(*sums, lead)


def on_device(tokens, norm_gain, qkv_weight, out_weight, log_decay):
    highest = lax.Precision.HIGHEST
    f32, bf16 = jnp.float32, jnp.bfloat16
    inv_root = DH ** (-0.5)
    rows, _ = tokens.shape
    head_width = qkv_weight.shape[2]
    local_heads = head_width // DH
    section_len = rows * 8

    w_q = lax.all_gather(qkv_weight[:, 0], "seq", axis=0, tiled=True)
    moved = move_out_weight(out_weight)

    tot = jnp.broadcast_to(log_decay.sum(axis=0)[:, None], (local_heads, DH))
    others = [send(tot, z_shift(k)) for k in (1, 2, 3)]
    c_in, c_row, lead, row_tot = row_weights([tot] + others)
    others = [send(row_tot, y_shift(k)) for k in (1, 2, 3)]
    c_y = rows_weights([row_tot] + others, lead)

    w_k, w_v = qkv_weight[:, 1], qkv_weight[:, 2]
    first_k, first_v = ring_gather(w_k, y_shift), ring_gather(w_v, z_shift)

    wide = tokens.astype(f32)
    mean_sq = jnp.mean(wide * wide, axis=-1, keepdims=True)
    normed = (wide * lax.rsqrt(mean_sq + eps_norm) * norm_gain).astype(bf16)
    mine = [normed] + [send(normed, x_shift(k)) for k in (1, 2, 3)]

    k_lo, k_hi, v_lo, v_hi = stack_pairs(first_k, first_v)

    def second(lo, hi, shift):
        lo1, hi3 = send(lo, shift(1)), send(hi, shift(3))
        hi1, lo3 = send(hi, shift(1)), send(lo, shift(3))
        far = [send(lo1, shift(1)), send(hi3, shift(3))]
        return [lo, hi, lo1, hi1, lo3, hi3], far

    near_k, far_k = second(k_lo, k_hi, z_shift)
    near_v, far_v = second(v_lo, v_hi, y_shift)

    log_decay, mine, _ = lax.optimization_barrier((log_decay, mine, (k_lo, v_lo)))
    theirs = [send(m, PARTNER) for m in mine]
    section = assemble(mine, theirs)

    cum_log = jnp.cumsum(log_decay, axis=0)
    last_log = cum_log[-1]
    head_log = cum_log.T
    steps = jnp.arange(section_len)
    causal = (steps[:, None] >= steps[None, :])[None, :, :]
    diffs = head_log[:, :, None] - head_log[:, None, :]
    decays = jnp.where(causal, jnp.exp(jnp.where(causal, diffs, 0.0)), 0.0)
    carried = jnp.exp(last_log[None, :] - cum_log)

    sums = partial_kv(section, near_k, near_v, NEAR)
    moved, _ = lax.optimization_barrier((moved, section))
    w_out = lax.all_gather(moved, "seq", axis=0, tiled=True).reshape(16, head_width, head_width)
    keys, values = partial_kv(section, far_k, far_v, FAR, sums)
    keys = keys.reshape(section_len, local_heads, DH)
    values = values.reshape(section_len, local_heads, DH)
    weighted_keys = keys.astype(f32) * carried[:, :, None]
    summary = jnp.einsum("shd,she->hde", weighted_keys, values.astype(f32), precision=highest)

    sum_bf = summary.astype(bf16)
    sums_z = [summary] + [send(sum_bf, z_shift(k)).astype(f32) for k in (1, 2, 3)]
    row_state = sum(c_row[k][:, None] * sums_z[k] for k in range(4))
    state_in = sum(c_in[k][:, None] * sums_z[k] for k in range(4))
    row_bf = row_state.astype(bf16)
    queries = jnp.dot(section, w_q, preferred_element_type=f32).astype(bf16)
    queries = queries.reshape(section_len, local_heads, DH)
    for k in (1, 2, 3):
        state_in = state_in + c_y[k][:, None] * send(row_bf, y_shift(k)).astype(f32)

    scores = jnp.einsum("thd,shd->hts", queries, keys, preferred_element_type=f32)
    pair = (scores * decays * inv_root).astype(bf16)
    intra = jnp.einsum("hts,shd->thd", pair, values, preferred_element_type=f32)
    cross = (
        jnp.exp(cum_log)[:, :, None]
        * inv_root
        * jnp.einsum("thd,hde->the", queries.astype(f32), state_in, precision=highest)
    )
    mixed = intra + cross
    mixed_sq = jnp.mean(mixed * mixed, axis=-1, keepdims=True)
    heads_out = (mixed * lax.rsqrt(mixed_sq + eps_norm)).astype(bf16).reshape(section_len, head_width)

    own = heads_out
    h1, h3, h2 = (send(own, x_shift(k)) for k in (1, 3, 2))
    p0, p1, p3, p2 = (send(h, PARTNER) for h in (own, h1, h3, h2))
    sums = heads_out_dots([(0, 0, own), (0, 1, p0), (1, 0, h1), (3, 0, h3)], w_out)
    parts = heads_out_dots([(2, 0, h2), (1, 1, p1), (3, 1, p3), (2, 1, p2)], w_out, sums)
    got = [parts[0]]
    for i in range(1, 8):
        k, flip = i // 2, i % 2
        to = [(q * 2 + c, ((q + k) % 4) * 2 + (c ^ flip)) for q in range(4) for c in range(2)]
        got.append(lax.ppermute(parts[i], "blk", to))
    return finish(tokens, got)


def solution(mesh):
    in_specs = (
        P(("seq", "blk"), None),
        P(),
        P("seq", None, "blk"),
        P("blk", "seq"),
        P("seq", "blk"),
    )
    out_specs = P(("seq", "blk"), None)

    return jax.shard_map(on_device, mesh=mesh, in_specs=in_specs, out_specs=out_specs, check_vma=False)
```
